32 devices in a mesh: seq: 4 (over z), fsdp: 8 (over y, x, core).
Axes of the slice: x: 2, y: 2, z: 4, core: 2. Of those that a mesh axis runs over, the one named last changes fastest.
Arguments:
- block_input: bfloat16 [4096, 1024], P(('seq', 'fsdp')), may hold values from -6 to 6
- out_grad: bfloat16 [4096, 1024], P(('seq', 'fsdp')), may hold values from -6 to 6
- attn_gain: bfloat16 [1024], P('fsdp'), may hold values from 0.5 to 1.5
- attn_shift: bfloat16 [1024], P('fsdp'), may hold values from -1.75 to 1.75
- qkv_weight: bfloat16 [1024, 3072], P('fsdp'), may hold values from -0.1875 to 0.1875
- query_bias: bfloat16 [1024], P('fsdp'), may hold values from -3 to 3
- value_bias: bfloat16 [1024], P('fsdp'), may hold values from -0.625 to 0.625
- out_weight: bfloat16 [1024, 1024], P('fsdp'), may hold values from -1.5 to 1.5
- out_bias: bfloat16 [1024], P('fsdp'), may hold values from -1.75 to 1.75
- mlp_gain: bfloat16 [1024], P('fsdp'), may hold values from 0.5 to 1.5
- mlp_shift: bfloat16 [1024], P('fsdp'), may hold values from -1.75 to 1.75
- fc_weight: bfloat16 [1024, 4096], P(None, 'fsdp'), may hold values from -0.1875 to 0.1875
- fc_bias: bfloat16 [4096], P('fsdp'), may hold values from -3 to 3
- proj_weight: bfloat16 [4096, 1024], P('fsdp'), may hold values from -0.09375 to 0.09375
- proj_bias: bfloat16 [1024], P('fsdp'), may hold values from -1.75 to 1.75
Outputs:
- block_output: bfloat16 [4096, 1024], P(('seq', 'fsdp'))
- input_grad: float32 [4096, 1024], P(('seq', 'fsdp'))
- grad_attn_gain: float32 [1024], P('fsdp')
- grad_attn_shift: float32 [1024], P('fsdp')
- grad_qkv_weight: float32 [1024, 3072], P('fsdp')
- grad_query_bias: float32 [1024], P('fsdp')
- grad_value_bias: float32 [1024], P('fsdp')
- grad_out_weight: float32 [1024, 1024], P('fsdp')
- grad_out_bias: float32 [1024], P('fsdp')
- grad_mlp_gain: float32 [1024], P('fsdp')
- grad_mlp_shift: float32 [1024], P('fsdp')
- grad_fc_weight: float32 [1024, 4096], P(None, 'fsdp')
- grad_fc_bias: float32 [4096], P('fsdp')
- grad_proj_weight: float32 [4096, 1024], P('fsdp')
- grad_proj_bias: float32 [1024], P('fsdp')
The draws below stay inside these ranges and needn't reach their ends.
All inputs are finite; a program needn't handle non-finite values.
Results may differ from the reference program's by a relative error of at most 0.02.
Values may be sent and summed in bfloat16 or wider, within the bound.
A program may use at most 192 MiB of HBM per device.

```python
import math
import jax
import jax.numpy as jnp
from jax import lax

HEADS = 16
HEAD_DIM = 64
D = 1024
FF = 4096
TOKENS = 4096


def shard_levels(own_key, extent, shards, smallest, top_value):
    factor_of, own = 1.0, jax.random.fold_in(own_key, 6)
    for dim, parts in shards:
        steps = jnp.exp(jax.random.uniform(jax.random.fold_in(own, dim), (parts,), jnp.float32, smallest / len(shards), top_value / len(shards)))
        factor_of = factor_of * jnp.repeat(steps, extent[dim] // parts).reshape([-1 if axis == dim else 1 for axis in range(len(extent))])
    return factor_of


def scatter_about(key, shape, scale, limit, shards=(), dtype=jnp.bfloat16):
    drawn = jax.random.normal(key, shape, jnp.float32) * scale
    if len(shards) > 0:
        drawn = shard_levels(key, shape, shards, -0.22, 0.18) * drawn
    return jnp.clip(drawn, min=-limit, max=limit).astype(dtype)


def setup_inputs(seed: int = 0) -> dict:
    key_list = jax.random.split(jax.random.key(seed), 16)
    return {
        "block_input": scatter_about(key_list[0], (TOKENS, D), 1.0, 6.0, ((0, 32),)),
        "out_grad": scatter_about(key_list[1], (TOKENS, D), 1.0, 6.0, ((0, 32),)),
        "attn_gain": jnp.clip(1.0 + 0.1 * jax.random.normal(key_list[2], (D,), jnp.float32), 0.5, 1.5).astype(jnp.bfloat16),
        "attn_shift": scatter_about(key_list[3], (D,), 0.3, 1.75, ((0, 8),)),
        "qkv_weight": scatter_about(key_list[4], (D, 3 * D), D ** -0.5, 0.1875, ((0, 8),)),
        "query_bias": scatter_about(key_list[5], (D,), 0.5, 3.0, ((0, 8),)),
        "value_bias": scatter_about(key_list[6], (D,), 0.1, 0.625, ((0, 8),)),
        "out_weight": scatter_about(key_list[7], (D, D), (max(1, D // 64)) ** -0.5, 1.5, ((0, 8),)),
        "out_bias": scatter_about(key_list[8], (D,), 0.3, 1.75, ((0, 8),)),
        "mlp_gain": jnp.clip(1.0 + 0.1 * jax.random.normal(key_list[9], (D,), jnp.float32), 0.5, 1.5).astype(jnp.bfloat16),
        "mlp_shift": scatter_about(key_list[10], (D,), 0.3, 1.75, ((0, 8),)),
        "fc_weight": scatter_about(key_list[11], (D, FF), D ** -0.5, 0.1875, ((1, 8),)),
        "fc_bias": scatter_about(key_list[12], (FF,), 0.5, 3.0, ((0, 8),)),
        "proj_weight": scatter_about(key_list[13], (FF, D), FF ** -0.5, 0.09375, ((0, 8),)),
        "proj_bias": scatter_about(key_list[14], (D,), 0.3, 1.75, ((0, 8),)),
    }


norm_eps = 1e-05
gelu_coef = 0.7978845608028654
cubic_coef = 0.044715

def norm_forward(values, gain_vec, shift_vec):
    centre = lax.optimization_barrier(jnp.mean(values, axis=-1, keepdims=True))
    centred = values - centre
    inv_scale = lax.rsqrt(lax.optimization_barrier(jnp.mean(centred * centred, axis=-1, keepdims=True)) + norm_eps)
    normed = centred * inv_scale
    return (normed, inv_scale, normed * gain_vec + shift_vec)

def norm_backward(upstream, normed, inv_scale, gain_vec):
    scaled = upstream * gain_vec
    return inv_scale * (scaled - lax.optimization_barrier(jnp.mean(scaled, axis=-1, keepdims=True)) - normed * lax.optimization_barrier(jnp.mean(scaled * normed, axis=-1, keepdims=True)))

def gelu_value(pre_act):
    return 0.5 * pre_act * (1.0 + jnp.tanh(gelu_coef * (pre_act + cubic_coef * pre_act * pre_act * pre_act)))

def gelu_slope(pre_act):
    tanh_val = jnp.tanh(gelu_coef * (pre_act + cubic_coef * pre_act * pre_act * pre_act))
    return 0.5 * (1.0 + tanh_val) + 0.5 * pre_act * (1.0 - tanh_val * tanh_val) * gelu_coef * (1.0 + 3.0 * cubic_coef * pre_act * pre_act)

def forward_head(inputs):
    query_h, key_h, value_h = inputs
    score_scale = 1.0 / math.sqrt(HEAD_DIM)
    block_rows = TOKENS // 8
    out_parts = []
    lse_parts = []
    for block_idx in range(8):
        row_low = block_idx * block_rows
        row_high = row_low + block_rows
        scores = jnp.dot(query_h[row_low:row_high], key_h[:row_high].T, preferred_element_type=jnp.float32) * score_scale
        visible = jnp.arange(row_high)[None, :] <= (row_low + jnp.arange(block_rows))[:, None]
        weights = jnp.where(visible, jnp.exp(scores), 0.0)
        summed = lax.optimization_barrier(jnp.sum(weights, axis=-1))
        weighted = jnp.dot(weights.astype(jnp.bfloat16), value_h[:row_high], preferred_element_type=jnp.float32)
        out_parts.append((weighted / summed[:, None]).astype(jnp.bfloat16))
        lse_parts.append(jnp.log(summed))
    return (jnp.concatenate(out_parts, axis=0), jnp.concatenate(lse_parts, axis=0))

def backward_head(inputs):
    query_h, key_h, value_h, dout_h, lse_h, delta_h = inputs
    score_scale = 1.0 / math.sqrt(HEAD_DIM)
    block_rows = TOKENS // 8
    key_acc = jnp.zeros((TOKENS, HEAD_DIM), jnp.float32)
    value_acc = jnp.zeros((TOKENS, HEAD_DIM), jnp.float32)
    query_parts = []
    for block_idx in range(8):
        row_low = block_idx * block_rows
        row_high = row_low + block_rows
        query_blk = query_h[row_low:row_high]
        dout_blk = dout_h[row_low:row_high]
        scores = jnp.dot(query_blk, key_h[:row_high].T, preferred_element_type=jnp.float32) * score_scale
        visible = jnp.arange(row_high)[None, :] <= (row_low + jnp.arange(block_rows))[:, None]
        probs = jnp.where(visible, jnp.exp(scores - lse_h[row_low:row_high][:, None]), 0.0)
        value_acc = value_acc.at[:row_high].add(jnp.dot(probs.astype(jnp.bfloat16).T, dout_blk, preferred_element_type=jnp.float32))
        prob_grad = jnp.dot(dout_blk, value_h[:row_high].T, preferred_element_type=jnp.float32)
        score_grad = (probs * (prob_grad - delta_h[row_low:row_high][:, None])).astype(jnp.bfloat16)
        query_parts.append(jnp.dot(score_grad, key_h[:row_high], preferred_element_type=jnp.float32) * score_scale)
        key_acc = key_acc.at[:row_high].add(jnp.dot(score_grad.T, query_blk, preferred_element_type=jnp.float32) * score_scale)
    return (jnp.concatenate(query_parts, axis=0), key_acc, value_acc)

def reference(block_input, out_grad, attn_gain, attn_shift, qkv_weight, query_bias, value_bias, out_weight, out_bias, mlp_gain, mlp_shift, fc_weight, fc_bias, proj_weight, proj_bias):
    x_vals = block_input.astype(jnp.float32)
    gain1 = attn_gain.astype(jnp.float32)
    gain2 = mlp_gain.astype(jnp.float32)
    normed1, rstd1, affine1 = norm_forward(x_vals, gain1, attn_shift.astype(jnp.float32))
    norm1_bf = affine1.astype(jnp.bfloat16)
    bias_row = jnp.concatenate([query_bias.astype(jnp.float32), jnp.zeros((D,), jnp.float32), value_bias.astype(jnp.float32)])
    qkv_bf = (jnp.dot(norm1_bf, qkv_weight, preferred_element_type=jnp.float32) + bias_row).astype(jnp.bfloat16)
    heads = qkv_bf.reshape(TOKENS, 3, HEADS, HEAD_DIM)
    query_all = jnp.transpose(heads[:, 0], (1, 0, 2))
    key_all = jnp.transpose(heads[:, 1], (1, 0, 2))
    value_all = jnp.transpose(heads[:, 2], (1, 0, 2))
    out_heads, lse_all = lax.map(forward_head, (query_all, key_all, value_all))
    attn_tok = jnp.transpose(out_heads, (1, 0, 2)).reshape(TOKENS, D)
    resid1 = x_vals + jnp.dot(attn_tok, out_weight, preferred_element_type=jnp.float32) + out_bias.astype(jnp.float32)
    normed2, rstd2, affine2 = norm_forward(resid1, gain2, mlp_shift.astype(jnp.float32))
    norm2_bf = affine2.astype(jnp.bfloat16)
    hidden_pre = jnp.dot(norm2_bf, fc_weight, preferred_element_type=jnp.float32) + fc_bias.astype(jnp.float32)
    hidden_bf = gelu_value(hidden_pre).astype(jnp.bfloat16)
    mlp_out = jnp.dot(hidden_bf, proj_weight, preferred_element_type=jnp.float32) + proj_bias.astype(jnp.float32)
    block_output = (resid1 + mlp_out).astype(jnp.bfloat16)
    grad_vals = out_grad.astype(jnp.float32)
    grad_proj_weight = jnp.dot(hidden_bf.T, out_grad, preferred_element_type=jnp.float32)
    grad_proj_bias = lax.optimization_barrier(jnp.sum(grad_vals, axis=0))
    hidden_grad = jnp.dot(out_grad, proj_weight.T, preferred_element_type=jnp.float32)
    pre_grad = (hidden_grad * gelu_slope(hidden_pre)).astype(jnp.bfloat16)
    grad_fc_weight = jnp.dot(norm2_bf.T, pre_grad, preferred_element_type=jnp.float32)
    grad_fc_bias = lax.optimization_barrier(jnp.sum(pre_grad.astype(jnp.float32), axis=0))
    norm2_grad = jnp.dot(pre_grad, fc_weight.T, preferred_element_type=jnp.float32)
    grad_mlp_gain = lax.optimization_barrier(jnp.sum(norm2_grad * normed2, axis=0))
    grad_mlp_shift = lax.optimization_barrier(jnp.sum(norm2_grad, axis=0))
    resid1_grad = grad_vals + norm_backward(norm2_grad, normed2, rstd2, gain2)
    resid1_bf = resid1_grad.astype(jnp.bfloat16)
    grad_out_weight = jnp.dot(attn_tok.T, resid1_bf, preferred_element_type=jnp.float32)
    grad_out_bias = lax.optimization_barrier(jnp.sum(resid1_grad, axis=0))
    attn_grad = jnp.dot(resid1_bf, out_weight.T, preferred_element_type=jnp.float32).astype(jnp.bfloat16)
    dout_all = jnp.transpose(attn_grad.reshape(TOKENS, HEADS, HEAD_DIM), (1, 0, 2))
    delta_all = lax.optimization_barrier(jnp.sum(dout_all.astype(jnp.float32) * out_heads.astype(jnp.float32), axis=-1))
    query_grad, key_grad, value_grad = lax.map(backward_head, (query_all, key_all, value_all, dout_all, lse_all, delta_all))
    stacked = jnp.stack([query_grad, key_grad, value_grad], axis=0)
    qkv_grad = jnp.transpose(stacked, (2, 0, 1, 3)).reshape(TOKENS, 3 * D).astype(jnp.bfloat16)
    grad_qkv_weight = jnp.dot(norm1_bf.T, qkv_grad, preferred_element_type=jnp.float32)
    qkv_grad_vals = qkv_grad.astype(jnp.float32)
    grad_query_bias = lax.optimization_barrier(jnp.sum(qkv_grad_vals[:, :D], axis=0))
    grad_value_bias = lax.optimization_barrier(jnp.sum(qkv_grad_vals[:, 2 * D:], axis=0))
    norm1_grad = jnp.dot(qkv_grad, qkv_weight.T, preferred_element_type=jnp.float32)
    grad_attn_gain = lax.optimization_barrier(jnp.sum(norm1_grad * normed1, axis=0))
    grad_attn_shift = lax.optimization_barrier(jnp.sum(norm1_grad, axis=0))
    input_grad = resid1_grad + norm_backward(norm1_grad, normed1, rstd1, gain1)
    return (block_output, input_grad, grad_attn_gain, grad_attn_shift, grad_qkv_weight, grad_query_bias, grad_value_bias, grad_out_weight, grad_out_bias, grad_mlp_gain, grad_mlp_shift, grad_fc_weight, grad_fc_bias, grad_proj_weight, grad_proj_bias)
```

```python
import functools
import math

import jax
import jax.numpy as jnp
from jax import lax
from jax.experimental import pallas as pl
from jax.experimental.pallas import tpu as pltpu
from jax.sharding import PartitionSpec as P

HEADS = 16
MESH = pl.DeviceIdType.MESH
BF = jnp.bfloat16
F32 = jnp.float32

norm_eps = 1e-05
gelu_coef = 0.7978845608028654
cubic_coef = 0.044715


def norm_stats(values):
    centre = jnp.mean(values, axis=-1, keepdims=True)
    centred = values - centre
    inv_scale = lax.rsqrt(jnp.mean(centred * centred, axis=-1, keepdims=True) + norm_eps)
    return centred * inv_scale, inv_scale


def norm_backward(upstream, normed, inv_scale, gain_vec):
    scaled = upstream * gain_vec
    return inv_scale * (
        scaled
        - jnp.mean(scaled, axis=-1, keepdims=True)
        - normed * jnp.mean(scaled * normed, axis=-1, keepdims=True)
    )


def peer_barrier(n, me, everyone):
    barrier = pltpu.get_barrier_semaphore()
    if everyone:
        for d in range(1, n):
            pl.semaphore_signal(
                barrier, inc=1, device_id={"fsdp": lax.rem(me + d, n)}, device_id_type=MESH
            )
        pl.semaphore_wait(barrier, n - 1)
        return
    core = lax.rem(me, 2)
    pl.semaphore_signal(
        barrier, inc=1, device_id={"fsdp": me + 1 - 2 * core}, device_id_type=MESH
    )
    for d in range(1, n // 2):
        pl.semaphore_signal(
            barrier, inc=1, device_id={"fsdp": lax.rem(me + 2 * d, n)}, device_id_type=MESH
        )
    pl.semaphore_wait(barrier, n // 2)


def exchange_kernel(n, n_gather, n_swap, *refs):
    k = n_gather + n_swap
    ins, outs, sems = refs[:k], refs[k : 2 * k], refs[2 * k :]
    me = lax.axis_index("fsdp")
    core = lax.rem(me, 2)
    partner = me + 1 - 2 * core
    peer_barrier(n, me, n_swap > 0)
    pending, arrivals = [], []
    for a in range(n_gather):
        x, o = ins[a], outs[a]
        rows = x.shape[0]
        send, recv, fsend, frecv, local = sems[5 * a : 5 * a + 5]

        def block(i, o=o, rows=rows):
            return o.at[pl.ds(pl.multiple_of(i * rows, rows), rows)]

        for d in range(1, n // 2):
            copy = pltpu.make_async_remote_copy(
                x, block(me), send.at[d], recv.at[d],
                device_id={"fsdp": lax.rem(me + 2 * d, n)}, device_id_type=MESH,
            )
            copy.start()
            arrivals.append((copy, block(lax.rem(me + n - 2 * d, n)), fsend.at[d], frecv.at[d]))
        copy = pltpu.make_async_remote_copy(
            x, block(me), fsend.at[0], frecv.at[0],
            device_id={"fsdp": partner}, device_id_type=MESH,
        )
        copy.start()
        pending.append(copy)
        own = pltpu.make_async_copy(x, block(me), local.at[0])
        own.start()
        pending.append(own)
    for b in range(n_swap):
        x, o = ins[n_gather + b], outs[n_gather + b]
        send, recv, local = sems[5 * n_gather + 3 * b : 5 * n_gather + 3 * b + 3]
        for d in range(1, n):
            to = lax.rem(me + d, n)
            copy = pltpu.make_async_remote_copy(
                x.at[to], o.at[me], send.at[d], recv.at[d],
                device_id={"fsdp": to}, device_id_type=MESH,
            )
            copy.start()
            pending.append(copy)
        own = pltpu.make_async_copy(x.at[me], o.at[me], local.at[0])
        own.start()
        pending.append(own)
    for copy, landed, fs, fr in arrivals:
        copy.wait_recv()
        onward = pltpu.make_async_remote_copy(
            landed, landed, fs, fr, device_id={"fsdp": partner}, device_id_type=MESH
        )
        onward.start()
        pending.append(onward)
    for copy, _, _, _ in arrivals:
        copy.wait_send()
    for copy in pending:
        copy.wait()


def exchange(n, cid, gathers, swaps=()):
    k = len(gathers) + len(swaps)
    dma = pltpu.SemaphoreType.DMA
    sems = []
    for _ in gathers:
        sems += [dma((n // 2,)), dma((n // 2,)), dma((n // 2,)), dma((n // 2,)), dma((1,))]
    for _ in swaps:
        sems += [dma((n,)), dma((n,)), dma((1,))]
    shapes = [jax.ShapeDtypeStruct((n * g.shape[0],) + g.shape[1:], g.dtype) for g in gathers]
    shapes += [jax.ShapeDtypeStruct(s.shape, s.dtype) for s in swaps]
    return pl.pallas_call(
        functools.partial(exchange_kernel, n, len(gathers), len(swaps)),
        out_shape=tuple(shapes),
        in_specs=[pl.BlockSpec(memory_space=pl.ANY)] * k,
        out_specs=tuple([pl.BlockSpec(memory_space=pl.ANY)] * k),
        scratch_shapes=sems,
        compiler_params=pltpu.CompilerParams(collective_id=cid, has_side_effects=True),
        name=f"exchange{cid}",
    )(*gathers, *swaps)


def scatter_kernel(n, p_ref, o_ref, mine, theirs, sums, came, lsem, psend, precv, send, recv):
    me = lax.axis_index("fsdp")
    core = lax.rem(me, 2)
    partner = me + 1 - 2 * core
    chips = n // 2
    chip = (me - core) // 2
    rows = o_ref.shape[0]
    peer_barrier(n, me, False)

    def block(i):
        return p_ref.at[pl.ds(pl.multiple_of(i * rows, rows), rows)]

    order = list(range(1, chips)) + [0]
    pairs = {}
    for d in order:
        to = lax.rem(chip + d, chips)
        give = pltpu.make_async_remote_copy(
            block(2 * to + 1 - core), theirs.at[d], psend.at[d], precv.at[d],
            device_id={"fsdp": partner}, device_id_type=MESH,
        )
        give.start()
        keep = pltpu.make_async_copy(block(2 * to + core), mine.at[d], lsem.at[d])
        keep.start()
        pairs[d] = (give, keep)
    sent = []
    for d in order:
        give, keep = pairs[d]
        keep.wait()
        give.wait_recv()
        if d:
            sums[d] = (mine[d].astype(F32) + theirs[d].astype(F32)).astype(BF)
            copy = pltpu.make_async_remote_copy(
                sums.at[d], came.at[d], send.at[d], recv.at[d],
                device_id={"fsdp": lax.rem(me + 2 * d, n)}, device_id_type=MESH,
            )
            copy.start()
            sent.append((d, copy))
        else:
            o_ref[...] = mine[0].astype(F32) + theirs[0].astype(F32)
    for d, copy in sent:
        copy.wait_recv()
        o_ref[...] += came[d].astype(F32)
    for _, copy in sent:
        copy.wait_send()
    for d in order:
        pairs[d][0].wait_send()


def scatter_sum(n, cid, partial):
    rows, cols = partial.shape[0] // n, partial.shape[1]
    chips = n // 2
    dma = pltpu.SemaphoreType.DMA
    buf = pltpu.VMEM((chips, rows, cols), BF)
    return pl.pallas_call(
        functools.partial(scatter_kernel, n),
        out_shape=jax.ShapeDtypeStruct((rows, cols), F32),
        in_specs=[pl.BlockSpec(memory_space=pl.ANY)],
        out_specs=pl.BlockSpec(memory_space=pltpu.VMEM),
        scratch_shapes=[buf, buf, buf, buf] + [dma((chips,))] * 5,
        compiler_params=pltpu.CompilerParams(collective_id=cid, has_side_effects=True),
        name=f"scatter{cid}",
    )(partial)


def lane_heads(shape, size):
    return lax.broadcasted_iota(jnp.int32, shape, 1) // size


def dot_nt(a, b):
    return lax.dot_general(a, b, (((1,), (1,)), ((), ())), preferred_element_type=F32)


def attn_fwd_kernel(nh, hs, bk, z_ref, q_ref, kv_ref, o_ref, lse_ref):
    bq, w = q_ref.shape
    start = z_ref[0] * (bq * pl.num_programs(0)) + pl.program_id(0) * bq
    heads = lane_heads((bq, w), hs)
    q = q_ref[...]
    qh = [jnp.where(heads == h, q, jnp.zeros_like(q)) for h in range(nh)]

    def step(j, carry, masked):
        rows = pl.ds(pl.multiple_of(j * bk, bk), bk)
        k = kv_ref[rows, :w]
        v = kv_ref[rows, w:]
        out = []
        for h in range(nh):
            acc, tot = carry[h]
            e = jnp.exp(dot_nt(qh[h], k))
            if masked:
                qp = start + lax.broadcasted_iota(jnp.int32, e.shape, 0)
                kp = j * bk + lax.broadcasted_iota(jnp.int32, e.shape, 1)
                e = jnp.where(kp <= qp, e, 0.0)
            tot = tot + jnp.sum(e, axis=1, keepdims=True)
            acc = acc + jnp.dot(e.astype(BF), v, preferred_element_type=F32)
            out.append((acc, tot))
        return tuple(out)

    init = tuple((jnp.zeros((bq, w), F32), jnp.zeros((bq, 1), F32)) for _ in range(nh))
    full = start // bk
    last = (start + bq + bk - 1) // bk
    carry = lax.fori_loop(0, full, lambda j, c: step(j, c, False), init)
    carry = lax.fori_loop(full, last, lambda j, c: step(j, c, True), carry)
    out = carry[0][0] / carry[0][1]
    lse = jnp.broadcast_to(jnp.log(carry[0][1]), (bq, w))
    for h in range(1, nh):
        out = jnp.where(heads == h, carry[h][0] / carry[h][1], out)
        lse = jnp.where(heads == h, jnp.log(carry[h][1]), lse)
    o_ref[...] = out.astype(BF)
    lse_ref[...] = lse


def attn_dq_kernel(nh, hs, bk, scale, z_ref, q_ref, do_ref, o_ref, lse_ref, kv_ref, dq_ref):
    bq, w = q_ref.shape
    start = z_ref[0] * (bq * pl.num_programs(0)) + pl.program_id(0) * bq
    heads = lane_heads((bq, w), hs)
    q = q_ref[...]
    do = do_ref[...]
    prod = do.astype(F32) * o_ref[...].astype(F32)
    qh = [jnp.where(heads == h, q, jnp.zeros_like(q)) for h in range(nh)]
    dh = [jnp.where(heads == h, do, jnp.zeros_like(do)) for h in range(nh)]
    lse = [
        jnp.max(jnp.where(heads == h, lse_ref[...], -jnp.inf), axis=1, keepdims=True)
        for h in range(nh)
    ]
    delta = [
        jnp.sum(jnp.where(heads == h, prod, 0.0), axis=1, keepdims=True) for h in range(nh)
    ]

    def step(j, carry, masked):
        rows = pl.ds(pl.multiple_of(j * bk, bk), bk)
        k = kv_ref[rows, :w]
        v = kv_ref[rows, w:]
        out = []
        for h in range(nh):
            p = jnp.exp(dot_nt(qh[h], k) - lse[h])
            if masked:
                qp = start + lax.broadcasted_iota(jnp.int32, p.shape, 0)
                kp = j * bk + lax.broadcasted_iota(jnp.int32, p.shape, 1)
                p = jnp.where(kp <= qp, p, 0.0)
            ds = (p * (dot_nt(dh[h], v) - delta[h])).astype(BF)
            out.append(carry[h] + jnp.dot(ds, k, preferred_element_type=F32))
        return tuple(out)

    init = tuple(jnp.zeros((bq, w), F32) for _ in range(nh))
    full = start // bk
    last = (start + bq + bk - 1) // bk
    carry = lax.fori_loop(0, full, lambda j, c: step(j, c, False), init)
    carry = lax.fori_loop(full, last, lambda j, c: step(j, c, True), carry)
    out = carry[0]
    for h in range(1, nh):
        out = jnp.where(heads == h, carry[h], out)
    dq_ref[...] = (out * scale).astype(BF)


def attn_dkv_kernel(nh, hs, bq, z_ref, kv_ref, q_ref, do_ref, lse_ref, delta_ref, dkv_ref):
    bk = kv_ref.shape[0]
    w = q_ref.shape[1]
    total = q_ref.shape[0]
    start = z_ref[0] * (bk * pl.num_programs(0)) + pl.program_id(0) * bk
    heads = lane_heads((bk, w), hs)
    k = kv_ref[:, :w]
    v = kv_ref[:, w:]
    kh = [jnp.where(heads == h, k, jnp.zeros_like(k)) for h in range(nh)]
    vh = [jnp.where(heads == h, v, jnp.zeros_like(v)) for h in range(nh)]

    def step(i, carry, masked):
        rows = pl.ds(pl.multiple_of(i * bq, bq), bq)
        q = q_ref[rows, :]
        do = do_ref[rows, :]
        lse = lse_ref[:, rows]
        delta = delta_ref[:, rows]
        out = []
        for h in range(nh):
            dk, dv = carry[h]
            p = jnp.exp(dot_nt(kh[h], q) - lse[h : h + 1])
            if masked:
                kp = start + lax.broadcasted_iota(jnp.int32, p.shape, 0)
                qp = i * bq + lax.broadcasted_iota(jnp.int32, p.shape, 1)
                p = jnp.where(kp <= qp, p, 0.0)
            dv = dv + jnp.dot(p.astype(BF), do, preferred_element_type=F32)
            ds = (p * (dot_nt(vh[h], do) - delta[h : h + 1])).astype(BF)
            dk = dk + jnp.dot(ds, q, preferred_element_type=F32)
            out.append((dk, dv))
        return tuple(out)

    init = tuple((jnp.zeros((bk, w), F32), jnp.zeros((bk, w), F32)) for _ in range(nh))
    first = start // bq
    clear = (start + bk + bq - 1) // bq
    carry = lax.fori_loop(first, clear, lambda i, c: step(i, c, True), init)
    carry = lax.fori_loop(clear, total // bq, lambda i, c: step(i, c, False), carry)
    dk, dv = carry[0]
    for h in range(1, nh):
        dk = jnp.where(heads == h, carry[h][0], dk)
        dv = jnp.where(heads == h, carry[h][1], dv)
    dkv_ref[:, :w] = dk.astype(BF)
    dkv_ref[:, w:] = dv.astype(BF)


def gridded(kernel, steps, blocks, wholes, outs, args):
    vm = pltpu.VMEM

    def cut(shape):
        return pl.BlockSpec((shape[0] // steps, shape[1]), lambda i, z: (i, 0), memory_space=vm)

    def whole(shape):
        return pl.BlockSpec(shape, lambda i, z: (0, 0), memory_space=vm)

    specs = [cut(a.shape) for a in blocks] + [whole(a.shape) for a in wholes]
    many = isinstance(outs, tuple)
    return pl.pallas_call(
        kernel,
        out_shape=outs,
        grid_spec=pltpu.PrefetchScalarGridSpec(
            num_scalar_prefetch=1,
            grid=(steps,),
            in_specs=specs,
            out_specs=tuple(cut(o.shape) for o in outs) if many else cut(outs.shape),
        ),
        compiler_params=pltpu.CompilerParams(vmem_limit_bytes=56 * 2**20),
    )(args, *blocks, *wholes)


def on_device(
    block_input, out_grad, attn_gain, attn_shift, qkv_weight, query_bias, value_bias,
    out_weight, out_bias, mlp_gain, mlp_shift, fc_weight, fc_bias, proj_weight, proj_bias,
):
    tok, width = block_input.shape
    n = lax.axis_size("fsdp")
    me = lax.axis_index("fsdp")
    z_arr = lax.axis_index("seq").astype(jnp.int32).reshape(1)
    hs = width // HEADS
    w = width // n
    nh = w // hs
    scale = 1.0 / math.sqrt(hs)
    piece = n * tok
    bq = 512

    vecs = jnp.stack([attn_gain, attn_shift, out_bias, mlp_gain, mlp_shift, proj_bias])
    vecs = jnp.pad(vecs, ((0, 10), (0, 0)))
    w_cut = jnp.transpose(qkv_weight.reshape(w, 3, n, w), (2, 0, 1, 3)).reshape(n, w, 3 * w)
    x_all, vec_all, w_mine = exchange(n, 1, (block_input, vecs), (w_cut,))
    g_all = lax.all_gather(out_grad, "fsdp", axis=0, tiled=True)
    w_mine = w_mine.reshape(width, 3 * w)
    full = jnp.transpose(vec_all.reshape(n, 16, w), (1, 0, 2)).reshape(16, width).astype(F32)
    gain1, shift1, out_b, gain2, shift2, proj_b = (full[i] for i in range(6))

    normed_all, _ = norm_stats(x_all.astype(F32))
    norm1 = (normed_all * gain1 + shift1).astype(BF)
    qkv = jnp.dot(norm1, w_mine, preferred_element_type=F32)
    q = (qkv[:, :w] + query_bias.astype(F32)).astype(BF) * jnp.asarray(scale, BF)
    bias_kv = jnp.concatenate([jnp.zeros((w,), F32), value_bias.astype(F32)])
    kv = (qkv[:, w:] + bias_kv).astype(BF)
    kv_all = lax.all_gather(kv, "seq", axis=0, tiled=True)
    q_all = lax.all_gather(q, "seq", axis=0, tiled=True)

    bf_w = jax.ShapeDtypeStruct((piece, w), BF)
    attn, lse = gridded(
        functools.partial(attn_fwd_kernel, nh, hs, bq), piece // bq, (q,), (kv_all,),
        (bf_w, jax.ShapeDtypeStruct((piece, w), F32)), z_arr,
    )
    o_all = lax.all_gather(attn, "seq", axis=0, tiled=True)
    lse_all = lax.all_gather(lse[:, ::hs].T, "seq", axis=1, tiled=True)

    part = jnp.dot(attn, out_weight, preferred_element_type=F32).astype(BF)
    x_vals = block_input.astype(F32)
    resid1 = x_vals + scatter_sum(n, 2, part) + out_b
    normed2, rstd2 = norm_stats(resid1)
    norm2 = (normed2 * gain2 + shift2).astype(BF)
    (norm2_all,) = exchange(n, 3, (norm2,))

    pre = jnp.dot(norm2_all, fc_weight, preferred_element_type=F32) + fc_bias.astype(F32)
    tanh_val = jnp.tanh(gelu_coef * (pre + cubic_coef * pre * pre * pre))
    hidden = (0.5 * pre * (1.0 + tanh_val)).astype(BF)
    slope = 0.5 * (1.0 + tanh_val) + 0.5 * pre * (1.0 - tanh_val * tanh_val) * gelu_coef * (
        1.0 + 3.0 * cubic_coef * pre * pre
    )
    hidden_grad = jnp.einsum("td,fd->tf", g_all, proj_weight, preferred_element_type=F32)
    pre_grad = (hidden_grad * slope).astype(BF)
    part = jnp.einsum("tf,df->td", pre_grad, fc_weight, preferred_element_type=F32).astype(BF)
    norm2_grad = scatter_sum(n, 4, part)

    grad_vals = out_grad.astype(F32)
    resid1_grad = grad_vals + norm_backward(norm2_grad, normed2, rstd2, gain2)
    (r_all,) = exchange(n, 5, (resid1_grad.astype(BF),))

    attn_grad = jnp.einsum("te,de->td", r_all, out_weight, preferred_element_type=F32).astype(BF)
    do_all = lax.all_gather(attn_grad, "seq", axis=0, tiled=True)
    dq = gridded(
        functools.partial(attn_dq_kernel, nh, hs, bq, scale), piece // bq,
        (q, attn_grad, attn, lse), (kv_all,), bf_w, z_arr,
    )

    mlp_part = jnp.dot(hidden, proj_weight, preferred_element_type=F32).astype(BF)
    g_proj = jnp.einsum("tf,td->fd", hidden, g_all, preferred_element_type=F32)
    g_fc = jnp.einsum("td,tf->df", norm2_all, pre_grad, preferred_element_type=F32)
    g_out = jnp.einsum("td,te->de", attn, r_all, preferred_element_type=F32)
    t_proj = lax.psum(g_proj.astype(BF), "seq").astype(F32)
    t_fc = lax.psum(g_fc.astype(BF), "seq").astype(F32)
    t_out = lax.psum(g_out.astype(BF), "seq").astype(F32)
    block_output = (resid1 + scatter_sum(n, 6, mlp_part) + proj_b).astype(BF)

    prod = do_all.astype(F32) * o_all.astype(F32)
    lane = jnp.arange(w) // hs
    delta_all = jnp.stack(
        [jnp.sum(jnp.where(lane == h, prod, 0.0), axis=1) for h in range(nh)]
    )
    dkv = gridded(
        functools.partial(attn_dkv_kernel, nh, hs, bq), piece // bq, (kv,),
        (q_all, do_all, lse_all, delta_all), jax.ShapeDtypeStruct((piece, 2 * w), BF), z_arr,
    )
    d_all = jnp.concatenate([dq, dkv], axis=1)
    part = jnp.einsum("tc,dc->td", d_all, w_mine, preferred_element_type=F32).astype(BF)
    norm1_grad = scatter_sum(n, 7, part)
    g_qkv = jnp.einsum("td,tc->dc", norm1, d_all, preferred_element_type=F32).astype(BF)
    (g_back,) = exchange(n, 8, (), (g_qkv.reshape(n, w, 3 * w),))
    g_back = lax.psum(g_back, "seq").astype(F32)
    t_qkv = jnp.transpose(g_back.reshape(n, w, 3, w), (1, 2, 0, 3)).reshape(w, 3 * width)

    normed1, rstd1 = norm_stats(x_vals)
    input_grad = resid1_grad + norm_backward(norm1_grad, normed1, rstd1, gain1)

    ff = fc_bias.shape[0] * n

    def slot(vec, size):
        return lax.dynamic_update_slice_in_dim(
            jnp.zeros((size,), F32), vec, me * vec.shape[0], 0
        )

    sums = [
        jnp.sum(norm1_grad * normed1, axis=0),
        jnp.sum(norm1_grad, axis=0),
        slot(jnp.sum(dq.astype(F32), axis=0), width),
        slot(jnp.sum(dkv[:, w:].astype(F32), axis=0), width),
        jnp.sum(resid1_grad, axis=0),
        jnp.sum(norm2_grad * normed2, axis=0),
        jnp.sum(norm2_grad, axis=0),
        slot(jnp.sum(pre_grad.astype(F32), axis=0), ff),
        jnp.sum(grad_vals, axis=0),
    ]
    joined = lax.psum(jnp.concatenate(sums), ("seq", "fsdp"))
    vec_out, at = [], 0
    for s in sums:
        size = s.shape[0]
        vec_out.append(lax.dynamic_slice_in_dim(joined, at + me * (size // n), size // n, 0))
        at += size
    a_gain, a_shift, q_b, v_b, o_b, m_gain, m_shift, f_b, p_b = vec_out
    return (
        block_output, input_grad, a_gain, a_shift, t_qkv, q_b, v_b, t_out, o_b,
        m_gain, m_shift, t_fc, f_b, t_proj, p_b,
    )


def solution(mesh):
    rows, vec, row, col = P(("seq", "fsdp"), None), P("fsdp"), P("fsdp", None), P(None, "fsdp")
    params = (vec, vec, row, vec, vec, row, vec, vec, vec, col, vec, row, vec)
    return jax.shard_map(
        on_device,
        mesh=mesh,
        in_specs=(rows, rows) + params,
        out_specs=(rows, rows) + params,
        check_vma=False,
    )
```

```python
import functools
import math

import jax
import jax.numpy as jnp
from jax import lax
from jax.experimental import pallas as pl
from jax.experimental.pallas import tpu as pltpu
from jax.sharding import PartitionSpec as P

HEADS = 16
MESH = pl.DeviceIdType.MESH
BF = jnp.bfloat16
F32 = jnp.float32

norm_eps = 1e-05
gelu_coef = 0.7978845608028654
cubic_coef = 0.044715


def norm_stats(values):
    centre = jnp.mean(values, axis=-1, keepdims=True)
    centred = values - centre
    inv_scale = lax.rsqrt(jnp.mean(centred * centred, axis=-1, keepdims=True) + norm_eps)
    return centred * inv_scale, inv_scale


def norm_backward(upstream, normed, inv_scale, gain_vec):
    scaled = upstream * gain_vec
    return inv_scale * (
        scaled
        - jnp.mean(scaled, axis=-1, keepdims=True)
        - normed * jnp.mean(scaled * normed, axis=-1, keepdims=True)
    )


def peer_barrier(n, me, everyone, g=1, mez=None):
    barrier = pltpu.get_barrier_semaphore()
    if everyone:
        for d in range(1, n):
            pl.semaphore_signal(
                barrier, inc=1, device_id={"fsdp": lax.rem(me + d, n)}, device_id_type=MESH
            )
        pl.semaphore_wait(barrier, n - 1)
        return
    core = lax.rem(me, 2)
    pl.semaphore_signal(
        barrier, inc=1, device_id={"fsdp": me + 1 - 2 * core}, device_id_type=MESH
    )
    for d in range(1, n // 2):
        pl.semaphore_signal(
            barrier, inc=1, device_id={"fsdp": lax.rem(me + 2 * d, n)}, device_id_type=MESH
        )
    for d in range(1, g):
        pl.semaphore_signal(
            barrier, inc=1, device_id={"seq": lax.rem(mez + d, g)}, device_id_type=MESH
        )
    pl.semaphore_wait(barrier, n // 2 + g - 1)


def exchange_kernel(n, n_gather, n_swap, *refs):
    k = n_gather + n_swap
    ins, outs, sems = refs[:k], refs[k : 2 * k], refs[2 * k :]
    me = lax.axis_index("fsdp")
    core = lax.rem(me, 2)
    partner = me + 1 - 2 * core
    peer_barrier(n, me, n_swap > 0)
    pending, arrivals = [], []
    for a in range(n_gather):
        x, o = ins[a], outs[a]
        rows = x.shape[0]
        send, recv, fsend, frecv, local = sems[5 * a : 5 * a + 5]

        def block(i, o=o, rows=rows):
            return o.at[pl.ds(pl.multiple_of(i * rows, rows), rows)]

        for d in range(1, n // 2):
            copy = pltpu.make_async_remote_copy(
                x, block(me), send.at[d], recv.at[d],
                device_id={"fsdp": lax.rem(me + 2 * d, n)}, device_id_type=MESH,
            )
            copy.start()
            arrivals.append((copy, block(lax.rem(me + n - 2 * d, n)), fsend.at[d], frecv.at[d]))
        copy = pltpu.make_async_remote_copy(
            x, block(me), fsend.at[0], frecv.at[0],
            device_id={"fsdp": partner}, device_id_type=MESH,
        )
        copy.start()
        pending.append(copy)
        own = pltpu.make_async_copy(x, block(me), local.at[0])
        own.start()
        pending.append(own)
    for b in range(n_swap):
        x, o = ins[n_gather + b], outs[n_gather + b]
        send, recv, local = sems[5 * n_gather + 3 * b : 5 * n_gather + 3 * b + 3]
        for d in range(1, n):
            to = lax.rem(me + d, n)
            copy = pltpu.make_async_remote_copy(
                x.at[to], o.at[me], send.at[d], recv.at[d],
                device_id={"fsdp": to}, device_id_type=MESH,
            )
            copy.start()
            pending.append(copy)
        own = pltpu.make_async_copy(x.at[me], o.at[me], local.at[0])
        own.start()
        pending.append(own)
    for copy, landed, fs, fr in arrivals:
        copy.wait_recv()
        onward = pltpu.make_async_remote_copy(
            landed, landed, fs, fr, device_id={"fsdp": partner}, device_id_type=MESH
        )
        onward.start()
        pending.append(onward)
    for copy, _, _, _ in arrivals:
        copy.wait_send()
    for copy in pending:
        copy.wait()


def exchange(n, cid, gathers, swaps=()):
    k = len(gathers) + len(swaps)
    dma = pltpu.SemaphoreType.DMA
    sems = []
    for _ in gathers:
        sems += [dma((n // 2,)), dma((n // 2,)), dma((n // 2,)), dma((n // 2,)), dma((1,))]
    for _ in swaps:
        sems += [dma((n,)), dma((n,)), dma((1,))]
    shapes = [jax.ShapeDtypeStruct((n * g.shape[0],) + g.shape[1:], g.dtype) for g in gathers]
    shapes += [jax.ShapeDtypeStruct(s.shape, s.dtype) for s in swaps]
    return pl.pallas_call(
        functools.partial(exchange_kernel, n, len(gathers), len(swaps)),
        out_shape=tuple(shapes),
        in_specs=[pl.BlockSpec(memory_space=pl.ANY)] * k,
        out_specs=tuple([pl.BlockSpec(memory_space=pl.ANY)] * k),
        scratch_shapes=sems,
        compiler_params=pltpu.CompilerParams(collective_id=cid, has_side_effects=True),
        name=f"exchange{cid}",
    )(*gathers, *swaps)


def scatter_body(n, p_ref, o_ref, mine, theirs, sums, came, lsem, psend, precv, send, recv):
    me = lax.axis_index("fsdp")
    core = lax.rem(me, 2)
    partner = me + 1 - 2 * core
    chips = n // 2
    chip = (me - core) // 2
    rows = o_ref.shape[0]

    def block(i):
        return p_ref.at[pl.ds(pl.multiple_of(i * rows, rows), rows)]

    order = list(range(1, chips)) + [0]
    pairs = {}
    for d in order:
        to = lax.rem(chip + d, chips)
        give = pltpu.make_async_remote_copy(
            block(2 * to + 1 - core), theirs.at[d], psend.at[d], precv.at[d],
            device_id={"fsdp": partner}, device_id_type=MESH,
        )
        give.start()
        keep = pltpu.make_async_copy(block(2 * to + core), mine.at[d], lsem.at[d])
        keep.start()
        pairs[d] = (give, keep)
    sent = []
    for d in order:
        give, keep = pairs[d]
        keep.wait()
        give.wait_recv()
        if d:
            sums[d] = (mine[d].astype(F32) + theirs[d].astype(F32)).astype(BF)
            copy = pltpu.make_async_remote_copy(
                sums.at[d], came.at[d], send.at[d], recv.at[d],
                device_id={"fsdp": lax.rem(me + 2 * d, n)}, device_id_type=MESH,
            )
            copy.start()
            sent.append((d, copy))
        else:
            o_ref[...] = mine[0].astype(F32) + theirs[0].astype(F32)
    for d, copy in sent:
        copy.wait_recv()
        o_ref[...] += came[d].astype(F32)
    for _, copy in sent:
        copy.wait_send()
    for d in order:
        pairs[d][0].wait_send()


def scatter_kernel(n, *refs):
    peer_barrier(n, lax.axis_index("fsdp"), False)
    scatter_body(n, *refs)


def tail_kernel(n, g, p_ref, gq_ref, o_ref, s_ref, *scratch):
    bufs, (zin, zlocal, zsend, zrecv) = scratch[:9], scratch[9:]
    me, mez = lax.axis_index("fsdp"), lax.axis_index("seq")
    peer_barrier(n, me, False, g, mez)
    own = pltpu.make_async_copy(gq_ref.at[mez], zin.at[0], zlocal.at[0])
    own.start()
    copies = []
    for d in range(1, g):
        to = lax.rem(mez + d, g)
        copy = pltpu.make_async_remote_copy(
            gq_ref.at[to], zin.at[d], zsend.at[d], zrecv.at[d],
            device_id={"seq": to}, device_id_type=MESH,
        )
        copy.start()
        copies.append(copy)
    scatter_body(n, p_ref, o_ref, *bufs)
    own.wait()
    for copy in copies:
        copy.wait()
    total = zin[0].astype(F32)
    for d in range(1, g):
        total = total + zin[d].astype(F32)
    s_ref[...] = total.astype(BF)


def tail_scatter(n, g, cid, partial, gq):
    rows, cols = partial.shape[0] // n, partial.shape[1]
    chips = n // 2
    dma = pltpu.SemaphoreType.DMA
    buf = pltpu.VMEM((chips, rows, cols), BF)
    return pl.pallas_call(
        functools.partial(tail_kernel, n, g),
        out_shape=(
            jax.ShapeDtypeStruct((rows, cols), F32), jax.ShapeDtypeStruct(gq.shape[1:], BF),
        ),
        in_specs=[pl.BlockSpec(memory_space=pl.ANY)] * 2,
        out_specs=(pl.BlockSpec(memory_space=pltpu.VMEM),) * 2,
        scratch_shapes=[buf, buf, buf, buf] + [dma((chips,))] * 5
        + [pltpu.VMEM(gq.shape, BF), dma((1,)), dma((g,)), dma((g,))],
        compiler_params=pltpu.CompilerParams(collective_id=cid, has_side_effects=True),
        name=f"tail{cid}",
    )(partial, gq)


def spread_kernel(n, g, s_ref, v_ref, out, vsum, came, *sems):
    vlocal, vsend, vrecv, slocal, ssend, srecv, fsend, frecv = sems
    me, mez = lax.axis_index("fsdp"), lax.axis_index("seq")
    barrier = pltpu.get_barrier_semaphore()
    others = [(dz, df) for dz in range(g) for df in range(n) if dz or df]

    def dev(dz, df):
        return {"seq": lax.rem(mez + dz, g), "fsdp": lax.rem(me + df, n)}

    for dz, df in others:
        pl.semaphore_signal(barrier, inc=1, device_id=dev(dz, df), device_id_type=MESH)
    pl.semaphore_wait(barrier, n * g - 1)
    pending = []
    for df in range(1, n):
        to = lax.rem(me + df, n)
        copy = pltpu.make_async_remote_copy(
            s_ref.at[to], out.at[mez, me], ssend.at[df], srecv.at[df],
            device_id={"fsdp": to}, device_id_type=MESH,
        )
        copy.start()
        pending.append(copy)
    own = pltpu.make_async_copy(s_ref.at[me], out.at[mez, me], slocal.at[0])
    own.start()
    vown = pltpu.make_async_copy(v_ref.at[me], came.at[0], vlocal.at[0])
    vown.start()
    vcopies = []
    for dz, df in others:
        i = dz * n + df
        copy = pltpu.make_async_remote_copy(
            v_ref.at[lax.rem(me + df, n)], came.at[i], vsend.at[i], vrecv.at[i],
            device_id=dev(dz, df), device_id_type=MESH,
        )
        copy.start()
        vcopies.append(copy)
    onward = []
    for df in range(n):
        if df:
            pending[df - 1].wait_recv()
        else:
            own.wait()
        landed = out.at[mez, lax.rem(me + n - df, n)]
        for dz in range(1, g):
            i = dz * n + df
            copy = pltpu.make_async_remote_copy(
                landed, landed, fsend.at[i], frecv.at[i],
                device_id={"seq": lax.rem(mez + dz, g)}, device_id_type=MESH,
            )
            copy.start()
            onward.append(copy)
    vown.wait()
    for copy in vcopies:
        copy.wait()
    vsum[...] = jnp.sum(came[...], axis=0)
    for copy in pending:
        copy.wait_send()
    for copy in onward:
        copy.wait()


def spread(n, g, cid, s, v):
    dma = pltpu.SemaphoreType.DMA
    return pl.pallas_call(
        functools.partial(spread_kernel, n, g),
        out_shape=(
            jax.ShapeDtypeStruct((g,) + s.shape, BF), jax.ShapeDtypeStruct(v.shape[1:], F32),
        ),
        in_specs=[pl.BlockSpec(memory_space=pl.ANY)] * 2,
        out_specs=(
            pl.BlockSpec(memory_space=pl.ANY), pl.BlockSpec(memory_space=pltpu.VMEM),
        ),
        scratch_shapes=[
            pltpu.VMEM((g * n,) + v.shape[1:], F32),
            dma((1,)), dma((g * n,)), dma((g * n,)),
            dma((1,)), dma((n,)), dma((n,)), dma((g * n,)), dma((g * n,)),
        ],
        compiler_params=pltpu.CompilerParams(collective_id=cid, has_side_effects=True),
        name=f"spread{cid}",
    )(s, v)


def rows_kernel(g, x_ref, o_ref, local, send, recv):
    mez = lax.axis_index("seq")
    cols = x_ref.shape[1]
    barrier = pltpu.get_barrier_semaphore()
    for d in range(1, g):
        pl.semaphore_signal(
            barrier, inc=1, device_id={"seq": lax.rem(mez + d, g)}, device_id_type=MESH
        )
    pl.semaphore_wait(barrier, g - 1)
    here = o_ref.at[:, pl.ds(pl.multiple_of(mez * cols, cols), cols)]
    own = pltpu.make_async_copy(x_ref, here, local.at[0])
    own.start()
    copies = []
    for d in range(1, g):
        copy = pltpu.make_async_remote_copy(
            x_ref, here, send.at[d], recv.at[d],
            device_id={"seq": lax.rem(mez + d, g)}, device_id_type=MESH,
        )
        copy.start()
        copies.append(copy)
    own.wait()
    for copy in copies:
        copy.wait()


def gather_rows(g, cid, x):
    dma = pltpu.SemaphoreType.DMA
    return pl.pallas_call(
        functools.partial(rows_kernel, g),
        out_shape=jax.ShapeDtypeStruct((x.shape[0], g * x.shape[1]), x.dtype),
        in_specs=[pl.BlockSpec(memory_space=pl.ANY)],
        out_specs=pl.BlockSpec(memory_space=pl.ANY),
        scratch_shapes=[dma((1,)), dma((g,)), dma((g,))],
        compiler_params=pltpu.CompilerParams(collective_id=cid, has_side_effects=True),
        name=f"rows{cid}",
    )(x)


def scatter_sum(n, cid, partial):
    rows, cols = partial.shape[0] // n, partial.shape[1]
    chips = n // 2
    dma = pltpu.SemaphoreType.DMA
    buf = pltpu.VMEM((chips, rows, cols), BF)
    return pl.pallas_call(
        functools.partial(scatter_kernel, n),
        out_shape=jax.ShapeDtypeStruct((rows, cols), F32),
        in_specs=[pl.BlockSpec(memory_space=pl.ANY)],
        out_specs=pl.BlockSpec(memory_space=pltpu.VMEM),
        scratch_shapes=[buf, buf, buf, buf] + [dma((chips,))] * 5,
        compiler_params=pltpu.CompilerParams(collective_id=cid, has_side_effects=True),
        name=f"scatter{cid}",
    )(partial)


def lane_heads(shape, size):
    return lax.broadcasted_iota(jnp.int32, shape, 1) // size


def dot_nt(a, b):
    return lax.dot_general(a, b, (((1,), (1,)), ((), ())), preferred_element_type=F32)


def attn_fwd_kernel(nh, hs, bk, z_ref, q_ref, kv_ref, o_ref, lse_ref):
    bq, w = q_ref.shape
    start = z_ref[0] * (bq * pl.num_programs(0)) + pl.program_id(0) * bq
    heads = lane_heads((bq, w), hs)
    q = q_ref[...]
    qh = [jnp.where(heads == h, q, jnp.zeros_like(q)) for h in range(nh)]

    def step(j, carry, masked):
        rows = pl.ds(pl.multiple_of(j * bk, bk), bk)
        k = kv_ref[rows, :w]
        v = kv_ref[rows, w:]
        out = []
        for h in range(nh):
            acc, tot = carry[h]
            e = jnp.exp(dot_nt(qh[h], k))
            if masked:
                qp = start + lax.broadcasted_iota(jnp.int32, e.shape, 0)
                kp = j * bk + lax.broadcasted_iota(jnp.int32, e.shape, 1)
                e = jnp.where(kp <= qp, e, 0.0)
            tot = tot + jnp.sum(e, axis=1, keepdims=True)
            acc = acc + jnp.dot(e.astype(BF), v, preferred_element_type=F32)
            out.append((acc, tot))
        return tuple(out)

    init = tuple((jnp.zeros((bq, w), F32), jnp.zeros((bq, 1), F32)) for _ in range(nh))
    full = start // bk
    last = (start + bq + bk - 1) // bk
    carry = lax.fori_loop(0, full, lambda j, c: step(j, c, False), init)
    carry = lax.fori_loop(full, last, lambda j, c: step(j, c, True), carry)
    out = carry[0][0] / carry[0][1]
    lse = jnp.broadcast_to(jnp.log(carry[0][1]), (bq, w))
    for h in range(1, nh):
        out = jnp.where(heads == h, carry[h][0] / carry[h][1], out)
        lse = jnp.where(heads == h, jnp.log(carry[h][1]), lse)
    o_ref[...] = out.astype(BF)
    lse_ref[...] = lse


def attn_dq_kernel(nh, hs, bk, scale, z_ref, q_ref, do_ref, o_ref, lse_ref, kv_ref, dq_ref):
    bq, w = q_ref.shape
    start = z_ref[0] * (bq * pl.num_programs(0)) + pl.program_id(0) * bq
    heads = lane_heads((bq, w), hs)
    q = q_ref[...]
    do = do_ref[...]
    prod = do.astype(F32) * o_ref[...].astype(F32)
    qh = [jnp.where(heads == h, q, jnp.zeros_like(q)) for h in range(nh)]
    dh = [jnp.where(heads == h, do, jnp.zeros_like(do)) for h in range(nh)]
    lse = [
        jnp.max(jnp.where(heads == h, lse_ref[...], -jnp.inf), axis=1, keepdims=True)
        for h in range(nh)
    ]
    delta = [
        jnp.sum(jnp.where(heads == h, prod, 0.0), axis=1, keepdims=True) for h in range(nh)
    ]

    def step(j, carry, masked):
        rows = pl.ds(pl.multiple_of(j * bk, bk), bk)
        k = kv_ref[rows, :w]
        v = kv_ref[rows, w:]
        out = []
        for h in range(nh):
            p = jnp.exp(dot_nt(qh[h], k) - lse[h])
            if masked:
                qp = start + lax.broadcasted_iota(jnp.int32, p.shape, 0)
                kp = j * bk + lax.broadcasted_iota(jnp.int32, p.shape, 1)
                p = jnp.where(kp <= qp, p, 0.0)
            ds = (p * (dot_nt(dh[h], v) - delta[h])).astype(BF)
            out.append(carry[h] + jnp.dot(ds, k, preferred_element_type=F32))
        return tuple(out)

    init = tuple(jnp.zeros((bq, w), F32) for _ in range(nh))
    full = start // bk
    last = (start + bq + bk - 1) // bk
    carry = lax.fori_loop(0, full, lambda j, c: step(j, c, False), init)
    carry = lax.fori_loop(full, last, lambda j, c: step(j, c, True), carry)
    out = carry[0]
    for h in range(1, nh):
        out = jnp.where(heads == h, carry[h], out)
    dq_ref[...] = (out * scale).astype(BF)


def attn_dkv_kernel(nh, hs, bq, z_ref, kv_ref, q_ref, do_ref, stat_ref, dkv_ref):
    bk = kv_ref.shape[0]
    w = q_ref.shape[1]
    total = q_ref.shape[0]
    start = z_ref[0] * (bk * pl.num_programs(0)) + pl.program_id(0) * bk
    heads = lane_heads((bk, w), hs)
    k = kv_ref[:, :w]
    v = kv_ref[:, w:]
    kh = [jnp.where(heads == h, k, jnp.zeros_like(k)) for h in range(nh)]
    vh = [jnp.where(heads == h, v, jnp.zeros_like(v)) for h in range(nh)]

    def step(i, carry, masked):
        rows = pl.ds(pl.multiple_of(i * bq, bq), bq)
        q = q_ref[rows, :]
        do = do_ref[rows, :]
        stat = stat_ref[:, rows]
        out = []
        for h in range(nh):
            dk, dv = carry[h]
            p = jnp.exp(dot_nt(kh[h], q) - stat[h : h + 1])
            if masked:
                kp = start + lax.broadcasted_iota(jnp.int32, p.shape, 0)
                qp = i * bq + lax.broadcasted_iota(jnp.int32, p.shape, 1)
                p = jnp.where(kp <= qp, p, 0.0)
            dv = dv + jnp.dot(p.astype(BF), do, preferred_element_type=F32)
            ds = (p * (dot_nt(vh[h], do) - stat[nh + h : nh + h + 1])).astype(BF)
            dk = dk + jnp.dot(ds, q, preferred_element_type=F32)
            out.append((dk, dv))
        return tuple(out)

    init = tuple((jnp.zeros((bk, w), F32), jnp.zeros((bk, w), F32)) for _ in range(nh))
    first = start // bq
    clear = (start + bk + bq - 1) // bq
    carry = lax.fori_loop(first, clear, lambda i, c: step(i, c, True), init)
    carry = lax.fori_loop(clear, total // bq, lambda i, c: step(i, c, False), carry)
    dk, dv = carry[0]
    for h in range(1, nh):
        dk = jnp.where(heads == h, carry[h][0], dk)
        dv = jnp.where(heads == h, carry[h][1], dv)
    dkv_ref[:, :w] = dk.astype(BF)
    dkv_ref[:, w:] = dv.astype(BF)


def gridded(kernel, steps, blocks, wholes, outs, args):
    vm = pltpu.VMEM

    def cut(shape):
        return pl.BlockSpec((shape[0] // steps, shape[1]), lambda i, z: (i, 0), memory_space=vm)

    def whole(shape):
        return pl.BlockSpec(shape, lambda i, z: (0, 0), memory_space=vm)

    specs = [cut(a.shape) for a in blocks] + [whole(a.shape) for a in wholes]
    many = isinstance(outs, tuple)
    return pl.pallas_call(
        kernel,
        out_shape=outs,
        grid_spec=pltpu.PrefetchScalarGridSpec(
            num_scalar_prefetch=1,
            grid=(steps,),
            in_specs=specs,
            out_specs=tuple(cut(o.shape) for o in outs) if many else cut(outs.shape),
        ),
        compiler_params=pltpu.CompilerParams(vmem_limit_bytes=56 * 2**20),
    )(args, *blocks, *wholes)


def on_device(
    block_input, out_grad, attn_gain, attn_shift, qkv_weight, query_bias, value_bias,
    out_weight, out_bias, mlp_gain, mlp_shift, fc_weight, fc_bias, proj_weight, proj_bias,
):
    tok, width = block_input.shape
    n, g = lax.axis_size("fsdp"), lax.axis_size("seq")
    me = lax.axis_index("fsdp")
    z_arr = lax.axis_index("seq").astype(jnp.int32).reshape(1)
    hs = width // HEADS
    w = width // n
    nh = w // hs
    scale = 1.0 / math.sqrt(hs)
    piece = n * tok
    bq = 512

    vecs = jnp.stack([attn_gain, attn_shift, out_bias, mlp_gain, mlp_shift, proj_bias])
    vecs = jnp.pad(vecs, ((0, 10), (0, 0)))
    w_cut = jnp.transpose(qkv_weight.reshape(w, 3, n, w), (2, 0, 1, 3)).reshape(n, w, 3 * w)
    x_all, vec_all, w_mine = exchange(n, 1, (block_input, vecs), (w_cut,))
    g_all = lax.all_gather(out_grad, "fsdp", axis=0, tiled=True)
    w_mine = w_mine.reshape(width, 3 * w)
    full = jnp.transpose(vec_all.reshape(n, 16, w), (1, 0, 2)).reshape(16, width).astype(F32)
    gain1, shift1, out_b, gain2, shift2, proj_b = (full[i] for i in range(6))

    normed_all, _ = norm_stats(x_all.astype(F32))
    norm1 = (normed_all * gain1 + shift1).astype(BF)
    qkv = jnp.dot(norm1, w_mine, preferred_element_type=F32)
    q = (qkv[:, :w] + query_bias.astype(F32)).astype(BF) * jnp.asarray(scale, BF)
    bias_kv = jnp.concatenate([jnp.zeros((w,), F32), value_bias.astype(F32)])
    kv = (qkv[:, w:] + bias_kv).astype(BF)
    kv_all = lax.all_gather(kv, "seq", axis=0, tiled=True)
    q_all = lax.all_gather(q, "seq", axis=0, tiled=True)

    bf_w = jax.ShapeDtypeStruct((piece, w), BF)
    attn, lse = gridded(
        functools.partial(attn_fwd_kernel, nh, hs, bq), piece // bq, (q,), (kv_all,),
        (bf_w, jax.ShapeDtypeStruct((piece, w), F32)), z_arr,
    )

    part = jnp.dot(attn, out_weight, preferred_element_type=F32).astype(BF)
    x_vals = block_input.astype(F32)
    resid1 = x_vals + scatter_sum(n, 2, part) + out_b
    normed2, rstd2 = norm_stats(resid1)
    norm2 = (normed2 * gain2 + shift2).astype(BF)
    (norm2_all,) = exchange(n, 3, (norm2,))

    pre = jnp.dot(norm2_all, fc_weight, preferred_element_type=F32) + fc_bias.astype(F32)
    tanh_val = jnp.tanh(gelu_coef * (pre + cubic_coef * pre * pre * pre))
    hidden = (0.5 * pre * (1.0 + tanh_val)).astype(BF)
    slope = 0.5 * (1.0 + tanh_val) + 0.5 * pre * (1.0 - tanh_val * tanh_val) * gelu_coef * (
        1.0 + 3.0 * cubic_coef * pre * pre
    )
    hidden_grad = jnp.einsum("td,fd->tf", g_all, proj_weight, preferred_element_type=F32)
    pre_grad = (hidden_grad * slope).astype(BF)
    part = jnp.einsum("tf,df->td", pre_grad, fc_weight, preferred_element_type=F32).astype(BF)
    norm2_grad = scatter_sum(n, 4, part)

    grad_vals = out_grad.astype(F32)
    resid1_grad = grad_vals + norm_backward(norm2_grad, normed2, rstd2, gain2)
    (r_all,) = exchange(n, 5, (resid1_grad.astype(BF),))

    attn_grad = jnp.einsum("te,de->td", r_all, out_weight, preferred_element_type=F32).astype(BF)
    do_all = lax.all_gather(attn_grad, "seq", axis=0, tiled=True)
    prod = attn_grad.astype(F32) * attn.astype(F32)
    lane = jnp.arange(w)
    stats = [jnp.sum(jnp.where(lane == h * hs, lse, 0.0), axis=1) for h in range(nh)]
    stats += [jnp.sum(jnp.where(lane // hs == h, prod, 0.0), axis=1) for h in range(nh)]
    stats += [jnp.zeros((piece,), F32)] * (-2 * nh % 8)
    stat_all = gather_rows(g, 6, jnp.stack(stats))
    dq = gridded(
        functools.partial(attn_dq_kernel, nh, hs, bq, scale), piece // bq,
        (q, attn_grad, attn, lse), (kv_all,), bf_w, z_arr,
    )

    mlp_part = jnp.dot(hidden, proj_weight, preferred_element_type=F32).astype(BF)
    g_proj = jnp.einsum("tf,td->fd", hidden, g_all, preferred_element_type=F32)
    g_fc = jnp.einsum("td,tf->df", norm2_all, pre_grad, preferred_element_type=F32)
    g_out = jnp.einsum("td,te->de", attn, r_all, preferred_element_type=F32)
    t_proj = lax.psum(g_proj.astype(BF), "seq").astype(F32)
    t_fc = lax.psum(g_fc.astype(BF), "seq").astype(F32)
    t_out = lax.psum(g_out.astype(BF), "seq").astype(F32)
    mlp_out = lax.psum_scatter(mlp_part, "fsdp", scatter_dimension=0, tiled=True)
    block_output = (resid1 + mlp_out.astype(F32) + proj_b).astype(BF)

    dkv = gridded(
        functools.partial(attn_dkv_kernel, nh, hs, bq), piece // bq, (kv,),
        (q_all, do_all, stat_all), jax.ShapeDtypeStruct((piece, 2 * w), BF), z_arr,
    )
    d_all = jnp.concatenate([dq, dkv], axis=1)
    part = jnp.einsum("tc,dc->td", d_all, w_mine, preferred_element_type=F32).astype(BF)
    g_qkv = jnp.einsum("td,tc->dc", norm1, d_all, preferred_element_type=F32).astype(BF)
    g_qkv = jnp.transpose(g_qkv.reshape(n, g, w // g, 3 * w), (1, 0, 2, 3))
    norm1_grad, g_part = tail_scatter(n, g, 7, part, g_qkv)

    normed1, rstd1 = norm_stats(x_vals)
    input_grad = resid1_grad + norm_backward(norm1_grad, normed1, rstd1, gain1)

    whole = jnp.stack([
        jnp.sum(norm1_grad * normed1, axis=0),
        jnp.sum(norm1_grad, axis=0),
        jnp.sum(resid1_grad, axis=0),
        jnp.sum(norm2_grad * normed2, axis=0),
        jnp.sum(norm2_grad, axis=0),
        jnp.sum(grad_vals, axis=0),
    ])
    own = jnp.concatenate([
        jnp.sum(dq.astype(F32), axis=0),
        jnp.sum(dkv[:, w:].astype(F32), axis=0),
        jnp.sum(pre_grad.astype(F32), axis=0),
    ]).reshape(-1, w)
    here = (jnp.arange(n) == me)[:, None, None]
    vec = jnp.concatenate(
        [jnp.transpose(whole.reshape(-1, n, w), (1, 0, 2)), jnp.where(here, own[None], 0.0)],
        axis=1,
    )
    vec = jnp.pad(vec, ((0, 0), (0, -vec.shape[1] % 8), (0, 0)))
    g_back, v = spread(n, g, 8, g_part, vec)
    t_qkv = jnp.transpose(g_back.reshape(g, n, w // g, 3, w), (0, 2, 3, 1, 4))
    t_qkv = t_qkv.reshape(w, 3 * width).astype(F32)
    f_b = v[8 : 6 + own.shape[0]].reshape(-1)
    return (
        block_output, input_grad, v[0], v[1], t_qkv, v[6], v[7], t_out, v[2],
        v[3], v[4], t_fc, f_b, t_proj, v[5],
    )


def solution(mesh):
    rows, vec, row, col = P(("seq", "fsdp"), None), P("fsdp"), P("fsdp", None), P(None, "fsdp")
    params = (vec, vec, row, vec, vec, row, vec, vec, vec, col, vec, row, vec)
    return jax.shard_map(
        on_device,
        mesh=mesh,
        in_specs=(rows, rows) + params,
        out_specs=(rows, rows) + params,
        check_vma=False,
    )
```
